32 devices in a mesh: parts: 2 (over x), wall: 16 (over z, y, core).
Axes of the slice: x: 2, y: 2, z: 4, core: 2. Of those that a mesh axis runs over, the one named last changes fastest.
Arguments:
- displacement: float32 [3, 524288], P(None, ('parts', 'wall')), parts along dimension 1, may hold values from -6 to 6
- velocity: float32 [3, 524288], P(None, ('parts', 'wall')), parts along dimension 1, may hold values from -6 to 6
- send_list: int32 [32, 16, 64], P(('parts', 'wall')), parts along dimension 0, may hold values from 0 to 16383, as said below
- arrive_list: int32 [32, 16, 64], P(('parts', 'wall')), parts along dimension 0, may hold values from 0 to 16383, as said below
- recv_count: int32 [32, 16], P(('parts', 'wall')), parts along dimension 0, may hold values from 0 to 64, as said below
- horizon_blocks: int32 [4096, 27], P(('parts', 'wall')), parts along dimension 0, may hold values from 0 to 2047, as said below
- bond_intact: int32 [4096, 27, 128], P(('parts', 'wall')), parts along dimension 0, may hold values 0 or 1
- modulus: float32 [524288], P(('parts', 'wall')), parts along dimension 0, may hold values from 0.5 to 2
- bond_weight: bfloat16 [27, 128, 128], replicated, may hold values from -0.109375 to 0.109375
Outputs:
- new_displacement: float32 [3, 524288], P(None, ('parts', 'wall')), parts along dimension 1
- new_velocity: float32 [3, 524288], P(None, ('parts', 'wall')), parts along dimension 1
The draws below stay inside these ranges and needn't reach their ends.
There are 2 independent parts, one for each index of `parts`. The reference program is written for one: setup_inputs(seed, part) draws one part's arguments, and reference() takes and returns one part's arrays. A program takes and returns all parts, laid end to end along the dimension named above; an argument that names none is the same for every part. Nothing has to cross between parts.
Inputs may be any that keep to these rules, and one draw needn't show every extreme that they name: For c < recv_count[d, s], send_list[s, d, c] is the local index on owner s of a node handed to owner d; the nodes that s hands away are distinct, and every owner hands away as many nodes as it receives. Other slots hold 0. For c < recv_count[d, s], arrive_list[d, s, c] is the local index on owner d where the c-th node from s lands; over all s and c these are exactly the local indices that d hands away, each once. Other slots hold 0. recv_count[d, s] is 0 for s = d and at least 1 otherwise; at most 64 nodes go from one owner to one other owner, and that many do on some pair in every draw. `horizon_blocks`: block b lies in layer b // 64; every block listed for b lies in the same layer, the layer before or the layer after.
All inputs are finite; a program needn't handle non-finite values. No bound on the sum of `bond_intact` on one device may be relied on, other than what follows from the above.
Results may differ from the reference program's by a relative error of at most 0.0011.
Values may be sent and summed in bfloat16 or wider, within the bound.
A program may use at most 64 MiB of HBM per device.

```python
import math
import jax
import jax.numpy as jnp
from jax import lax

BLK = 128
NNZ = 27
SUBSTEPS = 2
LAYER = 64
CAP = 64
NB_DEV = 128
NODES_DEV = 16384
NBLK = 2048
NODES = 262144
NLAYERS = 32
N_WALL = 16


def migration_plan(key):
    base_key = jax.random.fold_in(key, 7)
    key_order, key_count, key_vacate = jax.random.split(base_key, 3)
    ordering = jax.random.permutation(key_order, N_WALL).astype(jnp.int32)
    amounts = jax.random.randint(key_count, (N_WALL,), 1, CAP + 1, dtype=jnp.int32)
    amounts = amounts.at[0].set(0).at[1].set(CAP)
    starts = jnp.cumsum(amounts) - amounts
    vacate_keys = jax.random.split(key_vacate, N_WALL)

    def vacate_one(single):
        return jax.random.permutation(single, NODES_DEV)
    vacated = jax.vmap(vacate_one)(vacate_keys).astype(jnp.int32)
    offsets = (ordering[None, :] - ordering[:, None]) % N_WALL
    slot_ids = jnp.arange(CAP, dtype=jnp.int32)
    live_slot = slot_ids[None, None, :] < amounts[offsets][:, :, None]
    spot_ids = jnp.minimum(starts[offsets][:, :, None] + slot_ids[None, None, :], NODES_DEV - 1)
    owners = jnp.arange(N_WALL, dtype=jnp.int32)[:, None, None]
    sent_ids = jnp.where(live_slot, vacated[owners, spot_ids], 0).astype(jnp.int32)
    spot_turned = jnp.transpose(spot_ids, (1, 0, 2))
    live_turned = jnp.transpose(live_slot, (1, 0, 2))
    arrived = jnp.where(live_turned, vacated[owners, spot_turned], 0).astype(jnp.int32)
    received = amounts[jnp.transpose(offsets)].astype(jnp.int32)
    return (sent_ids, arrived, received)


def draw_send_list(key, part):
    return migration_plan(key)[0]


def draw_arrive_list(key, part):
    return migration_plan(key)[1]


def draw_recv_count(key, part):
    return migration_plan(key)[2]


def draw_horizon_blocks(key, part):
    key_layer, key_place = jax.random.split(jax.random.fold_in(key, 11))
    layer_ids = jnp.arange(NBLK, dtype=jnp.int32) // LAYER
    layer_step = jax.random.randint(key_layer, (NBLK, NNZ), -1, 2, dtype=jnp.int32)
    target_layer = jnp.clip(layer_ids[:, None] + layer_step, 0, NLAYERS - 1)
    position_in = jax.random.randint(key_place, (NBLK, NNZ), 0, LAYER, dtype=jnp.int32)
    return (target_layer * LAYER + position_in).astype(jnp.int32)


def set_ends(result, own_key, smallest, high):
    place = [jax.random.randint(jax.random.fold_in(own_key, axis), (), 0, length) for axis, length in enumerate(result.shape)]
    widest = result.shape.index(max(result.shape))
    next_to = place[:widest] + [(place[widest] + 1) % result.shape[widest]] + place[widest + 1:]
    return result.at[tuple(place)].set(smallest).at[tuple(next_to)].set(high)


def block_levels(key, shape, cuts, low, top_value):
    def one(dim, parts):
        draws = jax.random.uniform(jax.random.fold_in(jax.random.fold_in(key, 6), dim), (parts,), jnp.float32, low / len(cuts), top_value / len(cuts))
        return jnp.repeat(jnp.exp(draws), shape[dim] // parts).reshape((-1,) + (1,) * (len(shape) - dim - 1))

    gain = one(*cuts[0])
    for cut in cuts[1:]:
        gain = gain * one(*cut)
    return gain


def gaussian(key, extent, scale, most, pieces=(), held_as=jnp.bfloat16):
    gain = block_levels(key, extent, pieces, -0.22, 0.18) if pieces else 1.0
    entries = jax.random.normal(key, extent, jnp.float32) * scale * gain
    return jnp.minimum(jnp.maximum(entries, -most), most).astype(held_as)


def setup_inputs(seed: int = 0, part: int = 0) -> dict:
    seeds = jax.random.split(jax.random.key(seed), 10)
    own_keys = jax.random.split(jax.random.fold_in(seeds[9], part), 10)
    return {
        "displacement": gaussian(own_keys[0], (3, NODES), 1.0, 6.0, ((1, 16),), jnp.float32),
        "velocity": gaussian(own_keys[1], (3, NODES), 1.0, 6.0, ((1, 16),), jnp.float32),
        "send_list": draw_send_list(jax.random.fold_in(jax.random.fold_in(seeds[9], part), 71), part),
        "arrive_list": draw_arrive_list(jax.random.fold_in(jax.random.fold_in(seeds[9], part), 71), part),
        "recv_count": draw_recv_count(jax.random.fold_in(jax.random.fold_in(seeds[9], part), 71), part),
        "horizon_blocks": draw_horizon_blocks(jax.random.fold_in(jax.random.fold_in(seeds[9], part), 71), part),
        "bond_intact": set_ends((jax.random.randint(own_keys[6], (NBLK, NNZ, BLK), 0, 10) < 9).astype(jnp.int32), jax.random.fold_in(own_keys[6], 1), 0, 1),
        "modulus": jnp.clip(jnp.exp(math.log(2.0) - 1.3862944 * jax.random.uniform(own_keys[7], (NODES,), jnp.float32) ** block_levels(own_keys[7], (NODES,), ((0, 16),), -0.2, 0.2)), 0.5, 2.0),
        "bond_weight": gaussian(seeds[8], (NNZ, BLK, BLK), (NNZ * BLK) ** -0.5, 0.109375),
    }


TIME_STEP = 0.25


def migrate_nodes(stacked, send_list, arrive_list, recv_count):
    owner_ids = jnp.arange(N_WALL).astype(jnp.int32)
    source_ids = owner_ids[None, :, None] * NODES_DEV + jnp.transpose(send_list, (1, 0, 2)).astype(jnp.int32)
    live_slot = jnp.arange(CAP).astype(jnp.int32)[None, None, :] < recv_count[:, :, None]
    target_ids = jnp.where(live_slot, owner_ids[:, None, None] * NODES_DEV + arrive_list, NODES).astype(jnp.int32)
    moved = stacked[:, source_ids.reshape(-1)]
    return stacked.at[:, target_ids.reshape(-1)].set(moved, mode="drop")


def contract_blocks(source, horizon_blocks, intact_float, kernel_float):
    row_count = source.shape[0]

    def one_group(bundle):
        columns, intact = bundle
        picked = jnp.take(source, columns, axis=1).astype(jnp.float32)
        products = jnp.einsum("rbji,jki->rbjk", picked, kernel_float)
        return jnp.sum(products * intact[None], axis=2)

    grouped = lax.map(one_group, (horizon_blocks.reshape(N_WALL, NB_DEV, NNZ), intact_float.reshape(N_WALL, NB_DEV, NNZ, BLK)))
    return jnp.transpose(grouped, (1, 0, 2, 3)).reshape(row_count, NODES)


def force_of(position, modulus, stiffness, horizon_blocks, intact_float, kernel_float):
    rounded = lax.optimization_barrier(position.astype(jnp.bfloat16))
    widened = rounded.astype(jnp.float32)
    summed = contract_blocks(rounded.reshape(3, NBLK, BLK), horizon_blocks, intact_float, kernel_float)
    stretch = modulus * (summed - stiffness * widened)
    dilatation = jnp.mean(stretch, axis=0)
    soften = 1.0 / (1.0 + dilatation * dilatation)
    soft_low = lax.optimization_barrier(soften.astype(jnp.bfloat16))
    weighted = (soft_low.astype(jnp.float32) * widened).astype(jnp.bfloat16)
    packed = jnp.concatenate([weighted, soft_low[None]], axis=0)
    paired = contract_blocks(packed.reshape(4, NBLK, BLK), horizon_blocks, intact_float, kernel_float)
    return 0.5 * (modulus * (paired[:3] - widened * paired[3]) + soften * stretch)


def reference(displacement, velocity, send_list, arrive_list, recv_count, horizon_blocks, bond_intact, modulus, bond_weight):
    stacked = jnp.concatenate([displacement, velocity], axis=0)
    migrated = migrate_nodes(stacked, send_list, arrive_list, recv_count)
    position = migrated[:3]
    speed = migrated[3:]
    intact_float = bond_intact.astype(jnp.float32)
    kernel_float = bond_weight.astype(jnp.float32)
    row_totals = jnp.sum(kernel_float, axis=2)
    stiffness = jnp.sum(intact_float * row_totals[None], axis=1).reshape(NODES)
    acceleration = force_of(position, modulus, stiffness, horizon_blocks, intact_float, kernel_float)
    for substep in range(SUBSTEPS):
        position = position + TIME_STEP * speed + (0.5 * TIME_STEP * TIME_STEP) * acceleration
        following = force_of(position, modulus, stiffness, horizon_blocks, intact_float, kernel_float)
        speed = speed + (0.5 * TIME_STEP) * (acceleration + following)
        acceleration = following
    return position, speed
```

```python
import functools

import jax
import jax.numpy as jnp
from jax import lax
from jax.experimental import pallas as pl
from jax.experimental.pallas import tpu as pltpu
from jax.sharding import PartitionSpec as P

SUBSTEPS = 2
LAYER = 64
TIME_STEP = 0.25
MESH = pl.DeviceIdType.MESH
F32 = jnp.float32
BF16 = jnp.bfloat16


def force_kernel(
    blocks,
    width,
    nnz,
    hor_ref,
    intact_ref,
    mod_ref,
    wt_ref,
    pos_in,
    vel_in,
    pos_ref,
    vel_ref,
    onehot_ref,
    ext_ref,
    picked_ref,
    diag_ref,
    stiff_ref,
    acc_ref,
    stretch_ref,
    soften_ref,
    send_sem,
    recv_sem,
):
    me = lax.axis_index("wall")
    count = lax.axis_size("wall")
    reach = 3 * LAYER
    slots = 2 * (SUBSTEPS + 1)
    has_left = me > 0
    has_right = me < count - 1
    left = lax.rem(me + count - 1, count)
    right = lax.rem(me + 1, count)

    barrier = pltpu.get_barrier_semaphore()

    @pl.when(has_left)
    def _():
        pl.semaphore_signal(barrier, inc=1, device_id={"wall": left}, device_id_type=MESH)

    @pl.when(has_right)
    def _():
        pl.semaphore_signal(barrier, inc=1, device_id={"wall": right}, device_id_type=MESH)

    def halo_copy(slot, half, rows):
        wide = rows * width
        if half == 0:
            source = ext_ref.at[slot, pl.ds(LAYER, LAYER), pl.ds(0, wide)]
            target = ext_ref.at[slot, pl.ds(3 * LAYER, LAYER), pl.ds(0, wide)]
            device = left
        else:
            source = ext_ref.at[slot, pl.ds(2 * LAYER, LAYER), pl.ds(0, wide)]
            target = ext_ref.at[slot, pl.ds(0, LAYER), pl.ds(0, wide)]
            device = right
        return pltpu.make_async_remote_copy(
            src_ref=source,
            dst_ref=target,
            send_sem=send_sem.at[slot, half],
            recv_sem=recv_sem.at[slot, 1 - half],
            device_id={"wall": device},
            device_id_type=MESH,
        )

    def exists(half):
        return has_left if half == 0 else has_right

    def send(slot, half, rows):
        @pl.when(exists(half))
        def _():
            halo_copy(slot, half, rows).start()

    def wait_halo(slot, half, rows):
        @pl.when(exists(half))
        def _():
            halo_copy(slot, 1 - half, rows).wait_recv()

    def own(half):
        return pl.ds(half * LAYER, LAYER)

    def put(slot, half, row, value):
        ext_ref[slot, pl.ds(LAYER + half * LAYER, LAYER), pl.ds(row * width, width)] = value

    def get(slot, half, row):
        return ext_ref[slot, pl.ds(LAYER + half * LAYER, LAYER), pl.ds(row * width, width)].astype(F32)

    pos_ref[...] = pos_in[...]
    vel_ref[...] = vel_in[...]
    for half in range(2):
        for row in range(3):
            put(0, half, row, pos_in[row, own(half), :].astype(BF16))

    @pl.when(jnp.logical_not(has_left))
    def _():
        for slot in range(slots):
            ext_ref[slot, pl.ds(0, LAYER), :] = jnp.zeros((LAYER, 4 * width), BF16)

    @pl.when(jnp.logical_not(has_right))
    def _():
        for slot in range(slots):
            ext_ref[slot, pl.ds(3 * LAYER, LAYER), :] = jnp.zeros((LAYER, 4 * width), BF16)

    pl.semaphore_wait(barrier, has_left.astype(jnp.int32) + has_right.astype(jnp.int32))

    send(0, 0, 3)
    send(0, 1, 3)

    lanes = lax.broadcasted_iota(jnp.int32, (LAYER, reach), 1)
    for half in range(2):
        local = hor_ref[own(half), :] - (me * blocks - LAYER + half * LAYER)
        for j in range(nnz):
            hit = local[:, j : j + 1] == lanes
            onehot_ref[half, pl.ds(j * LAYER, LAYER), :] = jnp.where(hit, 1.0, 0.0).astype(BF16)

    stiff = jnp.zeros((blocks, width), F32)
    zero = jnp.zeros((width, width), BF16)
    ones = jnp.ones((16, width), BF16)
    for j in range(nnz):
        weight = wt_ref[j]
        diag_ref[j, pl.ds(0, width), pl.ds(0, width)] = weight
        diag_ref[j, pl.ds(width, width), pl.ds(width, width)] = weight
        diag_ref[j, pl.ds(0, width), pl.ds(width, width)] = zero
        diag_ref[j, pl.ds(width, width), pl.ds(0, width)] = zero
        totals = jnp.dot(ones, weight, preferred_element_type=F32)[0:1, :]
        stiff = stiff + intact_ref[j] * totals
    stiff_ref[...] = stiff

    group = 9 if nnz % 9 == 0 else nnz

    def contract(slot, rows, half):
        wide = rows * width
        source = ext_ref[slot, pl.ds(half * LAYER, reach), pl.ds(0, wide)]
        for start in range(0, nnz, group):
            part = pl.ds(start * LAYER, group * LAYER)
            picked_ref[part, pl.ds(0, wide)] = jnp.dot(
                onehot_ref[half, part, :], source, preferred_element_type=F32
            ).astype(BF16)
        sums = [jnp.zeros((LAYER, width), F32) for _ in range(rows)]
        for j in range(nnz):
            part = pl.ds(j * LAYER, LAYER)
            mask = intact_ref[j, own(half), :]
            weight = diag_ref[j]
            for pair in range(2):
                first = 2 * pair
                if first + 1 < rows:
                    product = jnp.dot(
                        picked_ref[part, pl.ds(first * width, 2 * width)], weight, preferred_element_type=F32
                    )
                    sums[first] = sums[first] + product[:, :width] * mask
                    sums[first + 1] = sums[first + 1] + product[:, width:] * mask
                else:
                    product = jnp.dot(
                        picked_ref[part, pl.ds(first * width, width)], wt_ref[j], preferred_element_type=F32
                    )
                    sums[first] = sums[first] + product * mask
        return sums

    def evaluation(t, carry):
        near, far = 2 * t, 2 * t + 1
        for half in (0, 1):
            wait_halo(near, half, 3)
            summed = contract(near, 3, half)
            scaling = mod_ref[own(half), :]
            stiffness = stiff_ref[own(half), :]
            rounded = [get(near, half, row) for row in range(3)]
            stretch = [scaling * (summed[row] - stiffness * rounded[row]) for row in range(3)]
            dilatation = (stretch[0] + stretch[1] + stretch[2]) / 3.0
            soften = 1.0 / (1.0 + dilatation * dilatation)
            soft_low = soften.astype(BF16)
            soft_wide = soft_low.astype(F32)
            for row in range(3):
                put(far, half, row, (soft_wide * rounded[row]).astype(BF16))
                stretch_ref[row, own(half), :] = stretch[row]
            put(far, half, 3, soft_low)
            soften_ref[own(half), :] = soften
            send(far, half, 4)
        for half in (1, 0):
            wait_halo(far, half, 4)
            paired = contract(far, 4, half)
            scaling = mod_ref[own(half), :]
            soften = soften_ref[own(half), :]
            for row in range(3):
                rounded = get(near, half, row)
                force = 0.5 * (
                    scaling * (paired[row] - rounded * paired[3]) + soften * stretch_ref[row, own(half), :]
                )

                @pl.when(t > 0)
                def _():
                    vel_ref[row, own(half), :] = vel_ref[row, own(half), :] + 0.5 * TIME_STEP * (
                        acc_ref[row, own(half), :] + force
                    )

                acc_ref[row, own(half), :] = force

            @pl.when(t < SUBSTEPS)
            def _():
                for row in range(3):
                    moved = (
                        pos_ref[row, own(half), :]
                        + TIME_STEP * vel_ref[row, own(half), :]
                        + 0.5 * TIME_STEP * TIME_STEP * acc_ref[row, own(half), :]
                    )
                    pos_ref[row, own(half), :] = moved
                    put(2 * t + 2, half, row, moved.astype(BF16))
                send(2 * t + 2, half, 3)

        return carry

    lax.fori_loop(0, SUBSTEPS + 1, evaluation, 0)

    for half in range(2):
        @pl.when(exists(half))
        def _():
            for slot in range(slots):
                halo_copy(slot, half, 3 if slot % 2 == 0 else 4).wait_send()


def forces(horizon, intact, modulus, weight_turned, position, velocity):
    nnz, blocks, width = intact.shape
    slots = 2 * (SUBSTEPS + 1)
    vmem = pl.BlockSpec(memory_space=pltpu.VMEM)
    shape = jax.ShapeDtypeStruct((3, blocks, width), F32)
    return pl.pallas_call(
        functools.partial(force_kernel, blocks, width, nnz),
        out_shape=(shape, shape),
        in_specs=[vmem] * 6,
        out_specs=(vmem, vmem),
        scratch_shapes=[
            pltpu.VMEM((2, nnz * LAYER, 3 * LAYER), BF16),
            pltpu.VMEM((slots, 4 * LAYER, 4 * width), BF16),
            pltpu.VMEM((nnz * LAYER, 4 * width), BF16),
            pltpu.VMEM((nnz, 2 * width, 2 * width), BF16),
            pltpu.VMEM((blocks, width), F32),
            pltpu.VMEM((3, blocks, width), F32),
            pltpu.VMEM((3, blocks, width), F32),
            pltpu.VMEM((blocks, width), F32),
            pltpu.SemaphoreType.DMA((slots, 2)),
            pltpu.SemaphoreType.DMA((slots, 2)),
        ],
        compiler_params=pltpu.CompilerParams(
            collective_id=0, has_side_effects=True, vmem_limit_bytes=48 * 1024 * 1024
        ),
        name="forces",
    )(horizon, intact, modulus, weight_turned, position, velocity)


def shards(
    displacement,
    velocity,
    send_list,
    arrive_list,
    recv_count,
    horizon_blocks,
    bond_intact,
    modulus,
    bond_weight,
):
    node_count = displacement.shape[1]
    block_count = horizon_blocks.shape[0]
    block_width = node_count // block_count
    capacity = send_list.shape[2]
    stacked_state = jnp.concatenate([displacement, velocity], axis=0)
    outgoing = jnp.take(stacked_state, send_list[0].reshape(-1), axis=1)
    incoming = lax.all_to_all(outgoing, "wall", split_axis=1, concat_axis=1, tiled=True)
    live_slot = jnp.arange(capacity, dtype=jnp.int32)[None, :] < recv_count[0][:, None]
    landing = jnp.where(live_slot, arrive_list[0], node_count).reshape(-1)
    stacked_state = stacked_state.at[:, landing].set(incoming, mode="drop")
    blocked = stacked_state.reshape(6, block_count, block_width)
    intact_turned = jnp.transpose(bond_intact.astype(F32), (1, 0, 2))
    final_position, final_speed = forces(
        horizon_blocks,
        intact_turned,
        modulus.reshape(block_count, block_width),
        jnp.transpose(bond_weight, (0, 2, 1)),
        blocked[:3],
        blocked[3:],
    )
    return (final_position.reshape(3, node_count), final_speed.reshape(3, node_count))


def solution(mesh):
    in_specs = (
        P(None, ("parts", "wall")),
        P(None, ("parts", "wall")),
        P(("parts", "wall"), None, None),
        P(("parts", "wall"), None, None),
        P(("parts", "wall"), None),
        P(("parts", "wall"), None),
        P(("parts", "wall"), None, None),
        P(("parts", "wall")),
        P(),
    )
    out_specs = (P(None, ("parts", "wall")), P(None, ("parts", "wall")))
    return jax.shard_map(shards, mesh=mesh, in_specs=in_specs, out_specs=out_specs, check_vma=False)
```

```python
import functools

import jax
import jax.numpy as jnp
from jax import lax
from jax.experimental import pallas as pl
from jax.experimental.pallas import tpu as pltpu
from jax.sharding import PartitionSpec as P

SUBSTEPS = 2
LAYER = 64
PEER_BATCH = 16
TIME_STEP = 0.25
MESH = pl.DeviceIdType.MESH
F32 = jnp.float32
BF16 = jnp.bfloat16


def force_kernel(
    blocks,
    width,
    nnz,
    peers,
    send_ref,
    arrive_ref,
    count_ref,
    hor_ref,
    bonds_ref,
    mod_ref,
    weight_ref,
    pos_in,
    vel_in,
    pos_ref,
    vel_ref,
    out_buf,
    in_buf,
    spread_ref,
    landed_ref,
    raw_ref,
    intact_ref,
    wt_ref,
    onehot_ref,
    ext_ref,
    picked_ref,
    diag_ref,
    stiff_ref,
    acc_ref,
    stretch_ref,
    soften_ref,
    send_sem,
    recv_sem,
    node_send_sem,
    node_recv_sem,
    bond_sem,
):
    me = lax.axis_index("wall")
    count = lax.axis_size("wall")
    reach = 3 * LAYER
    slots = 2 * (SUBSTEPS + 1)
    has_left = me > 0
    has_right = me < count - 1
    left = lax.rem(me + count - 1, count)
    right = lax.rem(me + 1, count)

    nodes = blocks * width
    capacity = send_ref.shape[1]
    shift = width.bit_length() - 1
    batch = min(PEER_BATCH, peers)
    lane_count = batch * capacity

    bond_copies = [
        pltpu.make_async_copy(bonds_ref.at[:, j, :], raw_ref.at[j], bond_sem.at[j]) for j in range(nnz)
    ]
    for copy in bond_copies:
        copy.start()

    barrier = pltpu.get_barrier_semaphore()

    def greet(step, carry):
        pl.semaphore_signal(
            barrier, inc=1, device_id={"wall": lax.rem(me + step, count)}, device_id_type=MESH
        )
        return carry

    lax.fori_loop(1, peers, greet, 0)

    def split(value):
        high = value.astype(BF16)
        low = (value - high.astype(F32)).astype(BF16)
        return high, low

    state = [pos_in, pos_in, pos_in, vel_in, vel_in, vel_in]

    def gather_batch(step, carry):
        rows = send_ref[pl.ds(step * batch, batch), :]
        index = jnp.concatenate([rows[i : i + 1, :] for i in range(batch)], axis=1)
        picked_rows = []
        tile = 256 if lane_count % 256 == 0 else lane_count
        splits = [jnp.concatenate(split(state[row][row % 3]), axis=1) for row in range(6)]
        for start in range(0, lane_count, tile):
            part = index[:, start : start + tile]
            of_node = lax.broadcasted_iota(jnp.int32, (width, tile), 0) == (part & (width - 1))
            of_block = lax.broadcasted_iota(jnp.int32, (blocks, tile), 0) == (part >> shift)
            column = jnp.where(of_node, 1.0, 0.0).astype(BF16)
            column = jnp.concatenate([column, column], axis=0)
            values = []
            for row in range(6):
                found = jnp.dot(splits[row], column, preferred_element_type=F32)
                values.append(jnp.sum(jnp.where(of_block, found, 0.0), axis=0, keepdims=True))
            picked_rows.append(jnp.concatenate(values, axis=0))
        picked = jnp.concatenate(picked_rows, axis=1)
        for i in range(batch):
            out_buf[step * batch + i, 0:6, 0:capacity] = picked[:, i * capacity : (i + 1) * capacity]
        return carry

    lax.fori_loop(0, peers // batch, gather_batch, 0)
    in_buf[me, :, :] = jnp.zeros(in_buf.shape[1:], F32)
    pl.semaphore_wait(barrier, peers - 1)

    def node_copy(step):
        peer = lax.rem(me + step, count)
        return pltpu.make_async_remote_copy(
            src_ref=out_buf.at[peer],
            dst_ref=in_buf.at[me],
            send_sem=node_send_sem.at[peer],
            recv_sem=node_recv_sem.at[me],
            device_id={"wall": peer},
            device_id_type=MESH,
        )

    def node_arrival(step):
        peer = lax.rem(me + step, count)
        return pltpu.make_async_remote_copy(
            src_ref=out_buf.at[peer],
            dst_ref=in_buf.at[peer],
            send_sem=node_send_sem.at[peer],
            recv_sem=node_recv_sem.at[peer],
            device_id={"wall": peer},
            device_id_type=MESH,
        )

    def start_nodes(step, carry):
        node_copy(step).start()
        return carry

    lax.fori_loop(1, peers, start_nodes, 0)

    lanes = lax.broadcasted_iota(jnp.int32, (LAYER, reach), 1)
    for half in range(2):
        local = hor_ref[pl.ds(half * LAYER, LAYER), :] - (me * blocks - LAYER + half * LAYER)
        for j in range(nnz):
            hit = local[:, j : j + 1] == lanes
            onehot_ref[half, pl.ds(j * LAYER, LAYER), :] = jnp.where(hit, 1.0, 0.0).astype(BF16)

    for copy in bond_copies:
        copy.wait()
    stiff = jnp.zeros((blocks, width), F32)
    zero = jnp.zeros((width, width), BF16)
    ones = jnp.ones((16, width), BF16)
    for j in range(nnz):
        weight = jnp.transpose(weight_ref[j])
        wt_ref[j] = weight
        diag_ref[j, pl.ds(0, width), pl.ds(0, width)] = weight
        diag_ref[j, pl.ds(width, width), pl.ds(width, width)] = weight
        diag_ref[j, pl.ds(0, width), pl.ds(width, width)] = zero
        diag_ref[j, pl.ds(width, width), pl.ds(0, width)] = zero
        totals = jnp.dot(ones, weight, preferred_element_type=F32)[0:1, :]
        intact = raw_ref[j].astype(F32)
        intact_ref[j] = intact
        stiff = stiff + intact * totals
    stiff_ref[...] = stiff

    def halo_copy(slot, half, rows):
        wide = rows * width
        if half == 0:
            source = ext_ref.at[slot, pl.ds(LAYER, LAYER), pl.ds(0, wide)]
            target = ext_ref.at[slot, pl.ds(3 * LAYER, LAYER), pl.ds(0, wide)]
            device = left
        else:
            source = ext_ref.at[slot, pl.ds(2 * LAYER, LAYER), pl.ds(0, wide)]
            target = ext_ref.at[slot, pl.ds(0, LAYER), pl.ds(0, wide)]
            device = right
        return pltpu.make_async_remote_copy(
            src_ref=source,
            dst_ref=target,
            send_sem=send_sem.at[slot, half],
            recv_sem=recv_sem.at[slot, 1 - half],
            device_id={"wall": device},
            device_id_type=MESH,
        )

    def exists(half):
        return has_left if half == 0 else has_right

    def send(slot, half, rows):
        @pl.when(exists(half))
        def _():
            halo_copy(slot, half, rows).start()

    def wait_halo(slot, half, rows):
        @pl.when(exists(half))
        def _():
            halo_copy(slot, 1 - half, rows).wait_recv()

    def own(half):
        return pl.ds(half * LAYER, LAYER)

    def put(slot, half, row, value):
        ext_ref[slot, pl.ds(LAYER + half * LAYER, LAYER), pl.ds(row * width, width)] = value

    def get(slot, half, row):
        return ext_ref[slot, pl.ds(LAYER + half * LAYER, LAYER), pl.ds(row * width, width)].astype(F32)

    @pl.when(jnp.logical_not(has_left))
    def _():
        for slot in range(slots):
            ext_ref[slot, pl.ds(0, LAYER), :] = jnp.zeros((LAYER, 4 * width), BF16)

    @pl.when(jnp.logical_not(has_right))
    def _():
        for slot in range(slots):
            ext_ref[slot, pl.ds(3 * LAYER, LAYER), :] = jnp.zeros((LAYER, 4 * width), BF16)

    def finish_nodes(step, carry):
        node_arrival(step).wait()
        return carry

    lax.fori_loop(1, peers, finish_nodes, 0)

    landed_ref[...] = jnp.zeros(landed_ref.shape, F32)

    def scatter_batch(step, carry):
        rows = arrive_ref[pl.ds(step * batch, batch), :]
        slot_ids = lax.broadcasted_iota(jnp.int32, (1, capacity), 1)
        index = jnp.concatenate(
            [
                jnp.where(slot_ids < count_ref[0, step * batch + i], rows[i : i + 1, :], nodes)
                for i in range(batch)
            ],
            axis=1,
        )
        values = jnp.concatenate(
            [in_buf[step * batch + i][0:6, 0:capacity] for i in range(batch)], axis=1
        )
        high, low = split(values)
        parts = [high.astype(F32), low.astype(F32)]
        of_node = lax.broadcasted_iota(jnp.int32, (width, lane_count), 0) == (index & (width - 1))
        of_block = lax.broadcasted_iota(jnp.int32, (blocks, lane_count), 0) == (index >> shift)
        column = jnp.where(of_node, 1.0, 0.0).astype(BF16)
        for row in range(6):
            for k in range(2):
                spread_ref[pl.ds((2 * row + k) * blocks, blocks), :] = jnp.where(
                    of_block, parts[k][row : row + 1, :], 0.0
                ).astype(BF16)
        spread_ref[pl.ds(12 * blocks, blocks), :] = jnp.where(of_block, 1.0, 0.0).astype(BF16)
        landed_ref[...] = landed_ref[...] + lax.dot_general(
            spread_ref[...], column, (((1,), (1,)), ((), ())), preferred_element_type=F32
        )
        return carry

    lax.fori_loop(0, peers // batch, scatter_batch, 0)

    for half in (0, 1):
        hit = landed_ref[pl.ds(12 * blocks + half * LAYER, LAYER), :] > 0.5
        for row in range(6):
            high = landed_ref[pl.ds(2 * row * blocks + half * LAYER, LAYER), :]
            low = landed_ref[pl.ds((2 * row + 1) * blocks + half * LAYER, LAYER), :]
            value = jnp.where(hit, high + low, state[row][row % 3, own(half), :])
            if row < 3:
                pos_ref[row, own(half), :] = value
                put(0, half, row, value.astype(BF16))
            else:
                vel_ref[row - 3, own(half), :] = value
        send(0, half, 3)

    group = 9 if nnz % 9 == 0 else nnz

    def contract(slot, rows, half):
        wide = rows * width
        source = ext_ref[slot, pl.ds(half * LAYER, reach), pl.ds(0, wide)]
        for start in range(0, nnz, group):
            part = pl.ds(start * LAYER, group * LAYER)
            picked_ref[part, pl.ds(0, wide)] = jnp.dot(
                onehot_ref[half, part, :], source, preferred_element_type=F32
            ).astype(BF16)
        sums = [jnp.zeros((LAYER, width), F32) for _ in range(rows)]
        for j in range(nnz):
            part = pl.ds(j * LAYER, LAYER)
            mask = intact_ref[j, own(half), :]
            weight = diag_ref[j]
            for pair in range(2):
                first = 2 * pair
                if first + 1 < rows:
                    product = jnp.dot(
                        picked_ref[part, pl.ds(first * width, 2 * width)], weight, preferred_element_type=F32
                    )
                    sums[first] = sums[first] + product[:, :width] * mask
                    sums[first + 1] = sums[first + 1] + product[:, width:] * mask
                else:
                    product = jnp.dot(
                        picked_ref[part, pl.ds(first * width, width)], wt_ref[j], preferred_element_type=F32
                    )
                    sums[first] = sums[first] + product * mask
        return sums

    def evaluation(t, carry):
        near, far = 2 * t, 2 * t + 1
        for half in (0, 1):
            wait_halo(near, half, 3)
            summed = contract(near, 3, half)
            scaling = mod_ref[own(half), :]
            stiffness = stiff_ref[own(half), :]
            rounded = [get(near, half, row) for row in range(3)]
            stretch = [scaling * (summed[row] - stiffness * rounded[row]) for row in range(3)]
            dilatation = (stretch[0] + stretch[1] + stretch[2]) / 3.0
            soften = 1.0 / (1.0 + dilatation * dilatation)
            soft_low = soften.astype(BF16)
            soft_wide = soft_low.astype(F32)
            for row in range(3):
                put(far, half, row, (soft_wide * rounded[row]).astype(BF16))
                stretch_ref[row, own(half), :] = stretch[row]
            put(far, half, 3, soft_low)
            soften_ref[own(half), :] = soften
            send(far, half, 4)
        for half in (1, 0):
            wait_halo(far, half, 4)
            paired = contract(far, 4, half)
            scaling = mod_ref[own(half), :]
            soften = soften_ref[own(half), :]
            for row in range(3):
                rounded = get(near, half, row)
                force = 0.5 * (
                    scaling * (paired[row] - rounded * paired[3]) + soften * stretch_ref[row, own(half), :]
                )

                @pl.when(t > 0)
                def _():
                    vel_ref[row, own(half), :] = vel_ref[row, own(half), :] + 0.5 * TIME_STEP * (
                        acc_ref[row, own(half), :] + force
                    )

                acc_ref[row, own(half), :] = force

            @pl.when(t < SUBSTEPS)
            def _():
                for row in range(3):
                    moved = (
                        pos_ref[row, own(half), :]
                        + TIME_STEP * vel_ref[row, own(half), :]
                        + 0.5 * TIME_STEP * TIME_STEP * acc_ref[row, own(half), :]
                    )
                    pos_ref[row, own(half), :] = moved
                    put(2 * t + 2, half, row, moved.astype(BF16))
                send(2 * t + 2, half, 3)

        return carry

    lax.fori_loop(0, SUBSTEPS + 1, evaluation, 0)

    for half in range(2):
        @pl.when(exists(half))
        def _():
            for slot in range(slots):
                halo_copy(slot, half, 3 if slot % 2 == 0 else 4).wait_send()


def shards(
    displacement,
    velocity,
    send_list,
    arrive_list,
    recv_count,
    horizon_blocks,
    bond_intact,
    modulus,
    bond_weight,
):
    node_count = displacement.shape[1]
    blocks, nnz, width = bond_intact.shape
    peers, capacity = send_list.shape[1:]
    lane_count = min(PEER_BATCH, peers) * capacity
    slots = 2 * (SUBSTEPS + 1)
    vmem = pl.BlockSpec(memory_space=pltpu.VMEM)
    smem = pl.BlockSpec(memory_space=pltpu.SMEM)
    anywhere = pl.BlockSpec(memory_space=pl.ANY)
    shape = jax.ShapeDtypeStruct((3, blocks, width), F32)
    final_position, final_speed = pl.pallas_call(
        functools.partial(force_kernel, blocks, width, nnz, peers),
        out_shape=(shape, shape),
        in_specs=[vmem, vmem, smem, vmem, anywhere, vmem, vmem, vmem, vmem],
        out_specs=(vmem, vmem),
        scratch_shapes=[
            pltpu.VMEM((peers, 8, 128 * pl.cdiv(capacity, 128)), F32),
            pltpu.VMEM((peers, 8, 128 * pl.cdiv(capacity, 128)), F32),
            pltpu.VMEM((13 * blocks, lane_count), BF16),
            pltpu.VMEM((13 * blocks, width), F32),
            pltpu.VMEM((nnz, blocks, width), jnp.int32),
            pltpu.VMEM((nnz, blocks, width), F32),
            pltpu.VMEM((nnz, width, width), BF16),
            pltpu.VMEM((2, nnz * LAYER, 3 * LAYER), BF16),
            pltpu.VMEM((slots, 4 * LAYER, 4 * width), BF16),
            pltpu.VMEM((nnz * LAYER, 4 * width), BF16),
            pltpu.VMEM((nnz, 2 * width, 2 * width), BF16),
            pltpu.VMEM((blocks, width), F32),
            pltpu.VMEM((3, blocks, width), F32),
            pltpu.VMEM((3, blocks, width), F32),
            pltpu.VMEM((blocks, width), F32),
            pltpu.SemaphoreType.DMA((slots, 2)),
            pltpu.SemaphoreType.DMA((slots, 2)),
            pltpu.SemaphoreType.DMA((peers,)),
            pltpu.SemaphoreType.DMA((peers,)),
            pltpu.SemaphoreType.DMA((nnz,)),
        ],
        compiler_params=pltpu.CompilerParams(
            collective_id=0, has_side_effects=True, vmem_limit_bytes=52 * 1024 * 1024
        ),
        name="forces",
    )(
        send_list[0],
        arrive_list[0],
        recv_count,
        horizon_blocks,
        bond_intact,
        modulus.reshape(blocks, width),
        bond_weight,
        displacement.reshape(3, blocks, width),
        velocity.reshape(3, blocks, width),
    )
    return (final_position.reshape(3, node_count), final_speed.reshape(3, node_count))


def solution(mesh):
    in_specs = (
        P(None, ("parts", "wall")),
        P(None, ("parts", "wall")),
        P(("parts", "wall"), None, None),
        P(("parts", "wall"), None, None),
        P(("parts", "wall"), None),
        P(("parts", "wall"), None),
        P(("parts", "wall"), None, None),
        P(("parts", "wall")),
        P(),
    )
    out_specs = (P(None, ("parts", "wall")), P(None, ("parts", "wall")))
    return jax.shard_map(shards, mesh=mesh, in_specs=in_specs, out_specs=out_specs, check_vma=False)
```

```python
import functools
import math

import jax
import jax.numpy as jnp
from jax import lax
from jax.experimental import pallas as pl
from jax.experimental.pallas import tpu as pltpu
from jax.sharding import PartitionSpec as P

SUBSTEPS = 2
LAYER = 64
PEER_BATCH = 16
TIME_STEP = 0.25
MESH = pl.DeviceIdType.MESH
F32 = jnp.float32
BF16 = jnp.bfloat16


def force_kernel(
    blocks,
    width,
    nnz,
    peers,
    send_ref,
    arrive_ref,
    count_ref,
    hor_ref,
    bonds_ref,
    mod_ref,
    weight_ref,
    pos_in,
    vel_in,
    pos_ref,
    vel_ref,
    out_buf,
    in_buf,
    spread_ref,
    landed_ref,
    raw_ref,
    intact_ref,
    wt_ref,
    onehot_ref,
    ext_ref,
    picked_ref,
    stiff_ref,
    acc_ref,
    stretch_ref,
    soften_ref,
    send_sem,
    recv_sem,
    node_send_sem,
    node_recv_sem,
    bond_sem,
):
    me = lax.axis_index("wall")
    count = lax.axis_size("wall")
    reach = 3 * LAYER
    slots = 2 * (SUBSTEPS + 1)
    has_left = me > 0
    has_right = me < count - 1
    left = lax.rem(me + count - 1, count)
    right = lax.rem(me + 1, count)

    nodes = blocks * width
    capacity = send_ref.shape[1]
    shift = width.bit_length() - 1
    batch = math.gcd(PEER_BATCH, peers)
    lane_count = batch * capacity

    bond_copy = pltpu.make_async_copy(bonds_ref, raw_ref, bond_sem)
    bond_copy.start()

    barrier = pltpu.get_barrier_semaphore()

    def greet(step, carry):
        pl.semaphore_signal(
            barrier, inc=1, device_id={"wall": lax.rem(me + step, count)}, device_id_type=MESH
        )
        return carry

    lax.fori_loop(1, peers, greet, 0)

    def split(value):
        high = value.astype(BF16)
        low = (value - high.astype(F32)).astype(BF16)
        return high, low

    state = [pos_in, pos_in, pos_in, vel_in, vel_in, vel_in]

    def gather_batch(step, carry):
        rows = send_ref[pl.ds(step * batch, batch), :]
        index = jnp.concatenate([rows[i : i + 1, :] for i in range(batch)], axis=1)
        picked_rows = []
        tile = 256 if lane_count % 256 == 0 else lane_count
        splits = [jnp.concatenate(split(state[row][row % 3]), axis=1) for row in range(6)]
        for start in range(0, lane_count, tile):
            part = index[:, start : start + tile]
            of_node = lax.broadcasted_iota(jnp.int32, (width, tile), 0) == (part & (width - 1))
            of_block = lax.broadcasted_iota(jnp.int32, (blocks, tile), 0) == (part >> shift)
            column = jnp.where(of_node, 1.0, 0.0).astype(BF16)
            column = jnp.concatenate([column, column], axis=0)
            values = []
            for row in range(6):
                found = jnp.dot(splits[row], column, preferred_element_type=F32)
                values.append(jnp.sum(jnp.where(of_block, found, 0.0), axis=0, keepdims=True))
            picked_rows.append(jnp.concatenate(values, axis=0))
        picked = jnp.concatenate(picked_rows, axis=1)
        for i in range(batch):
            out_buf[step * batch + i, 0:6, 0:capacity] = picked[:, i * capacity : (i + 1) * capacity]
        return carry

    lax.fori_loop(0, peers // batch, gather_batch, 0)
    in_buf[me, :, :] = jnp.zeros(in_buf.shape[1:], F32)
    pl.semaphore_wait(barrier, peers - 1)

    def node_copy(step):
        peer = lax.rem(me + step, count)
        return pltpu.make_async_remote_copy(
            src_ref=out_buf.at[peer],
            dst_ref=in_buf.at[me],
            send_sem=node_send_sem.at[peer],
            recv_sem=node_recv_sem.at[me],
            device_id={"wall": peer},
            device_id_type=MESH,
        )

    def node_arrival(step):
        peer = lax.rem(me + step, count)
        return pltpu.make_async_remote_copy(
            src_ref=out_buf.at[peer],
            dst_ref=in_buf.at[peer],
            send_sem=node_send_sem.at[peer],
            recv_sem=node_recv_sem.at[peer],
            device_id={"wall": peer},
            device_id_type=MESH,
        )

    def start_nodes(step, carry):
        node_copy(step).start()
        return carry

    lax.fori_loop(1, peers, start_nodes, 0)

    lanes = lax.broadcasted_iota(jnp.int32, (LAYER, reach), 1)
    padding = jnp.zeros((-nnz % 8, blocks), jnp.int32)
    horizon = jnp.transpose(jnp.concatenate([hor_ref[...], padding], axis=0))
    for half in range(2):
        local = horizon[half * LAYER : (half + 1) * LAYER] - (me * blocks - LAYER + half * LAYER)
        for j in range(nnz):
            hit = local[:, j : j + 1] == lanes
            onehot_ref[half, pl.ds(j * LAYER, LAYER), :] = jnp.where(hit, 1.0, 0.0).astype(BF16)

    bond_copy.wait()
    stiff = jnp.zeros((blocks, width), F32)
    ones = jnp.ones((16, width), BF16)
    for j in range(nnz):
        weight = jnp.transpose(weight_ref[j])
        wt_ref[j] = weight
        totals = jnp.dot(ones, weight, preferred_element_type=F32)[0:1, :]
        intact = raw_ref[j].astype(F32)
        intact_ref[j] = intact
        stiff = stiff + intact * totals
    stiff_ref[...] = stiff

    def halo_copy(slot, half, rows):
        wide = rows * width
        if half == 0:
            source = ext_ref.at[slot, pl.ds(LAYER, LAYER), pl.ds(0, wide)]
            target = ext_ref.at[slot, pl.ds(3 * LAYER, LAYER), pl.ds(0, wide)]
            device = left
        else:
            source = ext_ref.at[slot, pl.ds(2 * LAYER, LAYER), pl.ds(0, wide)]
            target = ext_ref.at[slot, pl.ds(0, LAYER), pl.ds(0, wide)]
            device = right
        return pltpu.make_async_remote_copy(
            src_ref=source,
            dst_ref=target,
            send_sem=send_sem.at[slot, half],
            recv_sem=recv_sem.at[slot, 1 - half],
            device_id={"wall": device},
            device_id_type=MESH,
        )

    def exists(half):
        return has_left if half == 0 else has_right

    def send(slot, half, rows):
        @pl.when(exists(half))
        def _():
            halo_copy(slot, half, rows).start()

    def wait_halo(slot, half, rows):
        @pl.when(exists(half))
        def _():
            halo_copy(slot, 1 - half, rows).wait_recv()

    def own(half):
        return pl.ds(half * LAYER, LAYER)

    def put(slot, half, row, value):
        ext_ref[slot, pl.ds(LAYER + half * LAYER, LAYER), pl.ds(row * width, width)] = value

    def get(slot, half, row):
        return ext_ref[slot, pl.ds(LAYER + half * LAYER, LAYER), pl.ds(row * width, width)].astype(F32)

    @pl.when(jnp.logical_not(has_left))
    def _():
        for slot in range(slots):
            ext_ref[slot, pl.ds(0, LAYER), :] = jnp.zeros((LAYER, 4 * width), BF16)

    @pl.when(jnp.logical_not(has_right))
    def _():
        for slot in range(slots):
            ext_ref[slot, pl.ds(3 * LAYER, LAYER), :] = jnp.zeros((LAYER, 4 * width), BF16)

    def finish_nodes(step, carry):
        node_arrival(step).wait()
        return carry

    lax.fori_loop(1, peers, finish_nodes, 0)

    landed_ref[...] = jnp.zeros(landed_ref.shape, F32)

    def scatter_batch(step, carry):
        rows = arrive_ref[pl.ds(step * batch, batch), :]
        slot_ids = lax.broadcasted_iota(jnp.int32, (1, capacity), 1)
        index = jnp.concatenate(
            [
                jnp.where(slot_ids < count_ref[0, step * batch + i], rows[i : i + 1, :], nodes)
                for i in range(batch)
            ],
            axis=1,
        )
        values = jnp.concatenate(
            [in_buf[step * batch + i][0:6, 0:capacity] for i in range(batch)], axis=1
        )
        high, low = split(values)
        parts = [high.astype(F32), low.astype(F32)]
        of_node = lax.broadcasted_iota(jnp.int32, (width, lane_count), 0) == (index & (width - 1))
        of_block = lax.broadcasted_iota(jnp.int32, (blocks, lane_count), 0) == (index >> shift)
        column = jnp.where(of_node, 1.0, 0.0).astype(BF16)
        for row in range(6):
            for k in range(2):
                spread_ref[pl.ds((2 * row + k) * blocks, blocks), :] = jnp.where(
                    of_block, parts[k][row : row + 1, :], 0.0
                ).astype(BF16)
        spread_ref[pl.ds(12 * blocks, blocks), :] = jnp.where(of_block, 1.0, 0.0).astype(BF16)
        landed_ref[...] = landed_ref[...] + lax.dot_general(
            spread_ref[...], column, (((1,), (1,)), ((), ())), preferred_element_type=F32
        )
        return carry

    lax.fori_loop(0, peers // batch, scatter_batch, 0)

    for half in (0, 1):
        hit = landed_ref[pl.ds(12 * blocks + half * LAYER, LAYER), :] > 0.5
        for row in range(6):
            high = landed_ref[pl.ds(2 * row * blocks + half * LAYER, LAYER), :]
            low = landed_ref[pl.ds((2 * row + 1) * blocks + half * LAYER, LAYER), :]
            value = jnp.where(hit, high + low, state[row][row % 3, own(half), :])
            if row < 3:
                pos_ref[row, own(half), :] = value
                put(0, half, row, value.astype(BF16))
            else:
                vel_ref[row - 3, own(half), :] = value
        send(0, half, 3)

    group = 9 if nnz % 9 == 0 else nnz

    def contract(slot, rows, half):
        wide = rows * width
        source = ext_ref[slot, pl.ds(half * LAYER, reach), pl.ds(0, wide)]
        for start in range(0, nnz, group):
            part = pl.ds(start * LAYER, group * LAYER)
            picked_ref[part, pl.ds(0, wide)] = jnp.dot(
                onehot_ref[half, part, :], source, preferred_element_type=F32
            ).astype(BF16)
        sums = [jnp.zeros((LAYER, width), F32) for _ in range(rows)]
        for j in range(nnz):
            part = pl.ds(j * LAYER, LAYER)
            mask = intact_ref[j, own(half), :]
            stacked = jnp.concatenate(
                [picked_ref[part, pl.ds(row * width, width)] for row in range(rows)], axis=0
            )
            product = jnp.dot(stacked, wt_ref[j], preferred_element_type=F32)
            for row in range(rows):
                sums[row] = sums[row] + product[row * LAYER : (row + 1) * LAYER] * mask
        return sums

    def evaluation(t, carry):
        near, far = 2 * t, 2 * t + 1
        for half in (0, 1):
            wait_halo(near, half, 3)
            summed = contract(near, 3, half)
            scaling = mod_ref[own(half), :]
            stiffness = stiff_ref[own(half), :]
            rounded = [get(near, half, row) for row in range(3)]
            stretch = [scaling * (summed[row] - stiffness * rounded[row]) for row in range(3)]
            dilatation = (stretch[0] + stretch[1] + stretch[2]) / 3.0
            soften = 1.0 / (1.0 + dilatation * dilatation)
            soft_low = soften.astype(BF16)
            soft_wide = soft_low.astype(F32)
            for row in range(3):
                put(far, half, row, (soft_wide * rounded[row]).astype(BF16))
                stretch_ref[row, own(half), :] = stretch[row]
            put(far, half, 3, soft_low)
            soften_ref[own(half), :] = soften
            send(far, half, 4)
        for half in (1, 0):
            wait_halo(far, half, 4)
            paired = contract(far, 4, half)
            scaling = mod_ref[own(half), :]
            soften = soften_ref[own(half), :]
            for row in range(3):
                rounded = get(near, half, row)
                force = 0.5 * (
                    scaling * (paired[row] - rounded * paired[3]) + soften * stretch_ref[row, own(half), :]
                )

                @pl.when(t > 0)
                def _():
                    vel_ref[row, own(half), :] = vel_ref[row, own(half), :] + 0.5 * TIME_STEP * (
                        acc_ref[row, own(half), :] + force
                    )

                acc_ref[row, own(half), :] = force

            @pl.when(t < SUBSTEPS)
            def _():
                for row in range(3):
                    moved = (
                        pos_ref[row, own(half), :]
                        + TIME_STEP * vel_ref[row, own(half), :]
                        + 0.5 * TIME_STEP * TIME_STEP * acc_ref[row, own(half), :]
                    )
                    pos_ref[row, own(half), :] = moved
                    put(2 * t + 2, half, row, moved.astype(BF16))
                send(2 * t + 2, half, 3)

        return carry

    lax.fori_loop(0, SUBSTEPS + 1, evaluation, 0)

    for half in range(2):
        @pl.when(exists(half))
        def _():
            for slot in range(slots):
                halo_copy(slot, half, 3 if slot % 2 == 0 else 4).wait_send()


def shards(
    displacement,
    velocity,
    send_list,
    arrive_list,
    recv_count,
    horizon_blocks,
    bond_intact,
    modulus,
    bond_weight,
):
    node_count = displacement.shape[1]
    blocks, nnz, width = bond_intact.shape
    peers, capacity = send_list.shape[1:]
    lane_count = math.gcd(PEER_BATCH, peers) * capacity
    slots = 2 * (SUBSTEPS + 1)
    vmem = pl.BlockSpec(memory_space=pltpu.VMEM)
    smem = pl.BlockSpec(memory_space=pltpu.SMEM)
    anywhere = pl.BlockSpec(memory_space=pl.ANY)
    shape = jax.ShapeDtypeStruct((3, blocks, width), F32)
    final_position, final_speed = pl.pallas_call(
        functools.partial(force_kernel, blocks, width, nnz, peers),
        out_shape=(shape, shape),
        in_specs=[vmem, vmem, smem, vmem, anywhere, vmem, vmem, vmem, vmem],
        out_specs=(vmem, vmem),
        scratch_shapes=[
            pltpu.VMEM((peers, 8, 128 * pl.cdiv(capacity, 128)), F32),
            pltpu.VMEM((peers, 8, 128 * pl.cdiv(capacity, 128)), F32),
            pltpu.VMEM((13 * blocks, lane_count), BF16),
            pltpu.VMEM((13 * blocks, width), F32),
            pltpu.VMEM((nnz, blocks, width), jnp.int32),
            pltpu.VMEM((nnz, blocks, width), F32),
            pltpu.VMEM((nnz, width, width), BF16),
            pltpu.VMEM((2, nnz * LAYER, 3 * LAYER), BF16),
            pltpu.VMEM((slots, 4 * LAYER, 4 * width), BF16),
            pltpu.VMEM((nnz * LAYER, 4 * width), BF16),
            pltpu.VMEM((blocks, width), F32),
            pltpu.VMEM((3, blocks, width), F32),
            pltpu.VMEM((3, blocks, width), F32),
            pltpu.VMEM((blocks, width), F32),
            pltpu.SemaphoreType.DMA((slots, 2)),
            pltpu.SemaphoreType.DMA((slots, 2)),
            pltpu.SemaphoreType.DMA((peers,)),
            pltpu.SemaphoreType.DMA((peers,)),
            pltpu.SemaphoreType.DMA,
        ],
        compiler_params=pltpu.CompilerParams(
            collective_id=0, has_side_effects=True, vmem_limit_bytes=52 * 1024 * 1024
        ),
        name="forces",
    )(
        send_list[0],
        arrive_list[0],
        recv_count,
        jnp.transpose(horizon_blocks),
        jnp.transpose(bond_intact, (1, 0, 2)),
        modulus.reshape(blocks, width),
        bond_weight,
        displacement.reshape(3, blocks, width),
        velocity.reshape(3, blocks, width),
    )
    return (final_position.reshape(3, node_count), final_speed.reshape(3, node_count))


def solution(mesh):
    in_specs = (
        P(None, ("parts", "wall")),
        P(None, ("parts", "wall")),
        P(("parts", "wall"), None, None),
        P(("parts", "wall"), None, None),
        P(("parts", "wall"), None),
        P(("parts", "wall"), None),
        P(("parts", "wall"), None, None),
        P(("parts", "wall")),
        P(),
    )
    out_specs = (P(None, ("parts", "wall")), P(None, ("parts", "wall")))
    return jax.shard_map(shards, mesh=mesh, in_specs=in_specs, out_specs=out_specs, check_vma=False)
```

```python
import functools
import math

import jax
import jax.numpy as jnp
from jax import lax
from jax.experimental import pallas as pl
from jax.experimental.pallas import tpu as pltpu
from jax.sharding import PartitionSpec as P

SUBSTEPS = 2
LAYER = 64
PEER_BATCH = 16
TIME_STEP = 0.25
MESH = pl.DeviceIdType.MESH
F32 = jnp.float32
BF16 = jnp.bfloat16


def force_kernel(
    blocks,
    width,
    nnz,
    peers,
    send_hbm,
    arrive_hbm,
    count_hbm,
    hor_hbm,
    bonds_hbm,
    mod_hbm,
    weight_hbm,
    pos_hbm,
    vel_hbm,
    pos_ref,
    vel_ref,
    send_ref,
    arrive_ref,
    count_ref,
    hor_ref,
    mod_ref,
    weight_ref,
    pos_raw,
    vel_raw,
    pos_in,
    vel_in,
    out_buf,
    in_buf,
    spread_ref,
    landed_ref,
    raw_ref,
    intact_ref,
    wt_ref,
    onehot_ref,
    ext_ref,
    picked_ref,
    stiff_ref,
    acc_ref,
    stretch_ref,
    soften_ref,
    send_sem,
    recv_sem,
    node_send_sem,
    node_recv_sem,
    fetch_sem,
):
    me = lax.axis_index("wall")
    count = lax.axis_size("wall")
    reach = 3 * LAYER
    slots = 2 * (SUBSTEPS + 1)
    has_left = me > 0
    has_right = me < count - 1
    left = lax.rem(me + count - 1, count)
    right = lax.rem(me + 1, count)

    nodes = blocks * width
    capacity = send_ref.shape[1]
    shift = width.bit_length() - 1
    batch = math.gcd(PEER_BATCH, peers)
    lane_count = batch * capacity

    pairs = [(send_hbm.at[0], send_ref)]
    pairs += [(pos_hbm, pos_raw), (vel_hbm, vel_raw)]
    early = len(pairs)
    pairs += [(hor_hbm, hor_ref), (weight_hbm, weight_ref), (bonds_hbm, raw_ref)]
    pairs += [(arrive_hbm.at[0], arrive_ref), (count_hbm, count_ref), (mod_hbm, mod_ref)]
    fetches = [pltpu.make_async_copy(pair[0], pair[1], fetch_sem.at[i]) for i, pair in enumerate(pairs)]
    for fetch in fetches:
        fetch.start()

    barrier = pltpu.get_barrier_semaphore()

    def greet(step, carry):
        pl.semaphore_signal(
            barrier, inc=1, device_id={"wall": lax.rem(me + step, count)}, device_id_type=MESH
        )
        return carry

    lax.fori_loop(1, peers, greet, 0)

    def split(value):
        high = value.astype(BF16)
        low = (value - high.astype(F32)).astype(BF16)
        return high, low

    for fetch in fetches[:early]:
        fetch.wait()
    for row in range(3):
        pos_in[row] = pos_raw[:, row, :]
        vel_in[row] = vel_raw[:, row, :]
    state = [pos_in, pos_in, pos_in, vel_in, vel_in, vel_in]

    def gather_batch(step, carry):
        rows = send_ref[pl.ds(step * batch, batch), :]
        index = jnp.concatenate([rows[i : i + 1, :] for i in range(batch)], axis=1)
        picked_rows = []
        tile = 256 if lane_count % 256 == 0 else lane_count
        splits = [jnp.concatenate(split(state[row][row % 3]), axis=1) for row in range(6)]
        for start in range(0, lane_count, tile):
            part = index[:, start : start + tile]
            of_node = lax.broadcasted_iota(jnp.int32, (width, tile), 0) == (part & (width - 1))
            of_block = lax.broadcasted_iota(jnp.int32, (blocks, tile), 0) == (part >> shift)
            column = jnp.where(of_node, 1.0, 0.0).astype(BF16)
            column = jnp.concatenate([column, column], axis=0)
            values = []
            for row in range(6):
                found = jnp.dot(splits[row], column, preferred_element_type=F32)
                values.append(jnp.sum(jnp.where(of_block, found, 0.0), axis=0, keepdims=True))
            picked_rows.append(jnp.concatenate(values, axis=0))
        picked = jnp.concatenate(picked_rows, axis=1)
        for i in range(batch):
            out_buf[step * batch + i, 0:6, 0:capacity] = picked[:, i * capacity : (i + 1) * capacity]
        return carry

    lax.fori_loop(0, peers // batch, gather_batch, 0)
    in_buf[me, :, :] = jnp.zeros(in_buf.shape[1:], F32)
    pl.semaphore_wait(barrier, peers - 1)

    def node_copy(step):
        peer = lax.rem(me + step, count)
        return pltpu.make_async_remote_copy(
            src_ref=out_buf.at[peer],
            dst_ref=in_buf.at[me],
            send_sem=node_send_sem.at[peer],
            recv_sem=node_recv_sem.at[me],
            device_id={"wall": peer},
            device_id_type=MESH,
        )

    def node_arrival(step):
        peer = lax.rem(me + step, count)
        return pltpu.make_async_remote_copy(
            src_ref=out_buf.at[peer],
            dst_ref=in_buf.at[peer],
            send_sem=node_send_sem.at[peer],
            recv_sem=node_recv_sem.at[peer],
            device_id={"wall": peer},
            device_id_type=MESH,
        )

    def start_nodes(step, carry):
        node_copy(step).start()
        return carry

    lax.fori_loop(1, peers, start_nodes, 0)

    lanes = lax.broadcasted_iota(jnp.int32, (LAYER, reach), 1)
    fetches[early].wait()
    padding = jnp.zeros((-nnz % 8, blocks), jnp.int32)
    horizon = jnp.transpose(jnp.concatenate([hor_ref[...], padding], axis=0))
    for half in range(2):
        local = horizon[half * LAYER : (half + 1) * LAYER] - (me * blocks - LAYER + half * LAYER)
        for j in range(nnz):
            hit = local[:, j : j + 1] == lanes
            onehot_ref[half, pl.ds(j * LAYER, LAYER), :] = jnp.where(hit, 1.0, 0.0).astype(BF16)

    for fetch in fetches[early + 1 :]:
        fetch.wait()
    stiff = jnp.zeros((blocks, width), F32)
    ones = jnp.ones((16, width), BF16)
    for j in range(nnz):
        weight = jnp.transpose(weight_ref[j])
        wt_ref[j] = weight
        totals = jnp.dot(ones, weight, preferred_element_type=F32)[0:1, :]
        intact = raw_ref[j].astype(F32)
        intact_ref[j] = intact
        stiff = stiff + intact * totals
    stiff_ref[...] = stiff

    def halo_copy(slot, half, rows):
        wide = rows * width
        if half == 0:
            source = ext_ref.at[slot, pl.ds(LAYER, LAYER), pl.ds(0, wide)]
            target = ext_ref.at[slot, pl.ds(3 * LAYER, LAYER), pl.ds(0, wide)]
            device = left
        else:
            source = ext_ref.at[slot, pl.ds(2 * LAYER, LAYER), pl.ds(0, wide)]
            target = ext_ref.at[slot, pl.ds(0, LAYER), pl.ds(0, wide)]
            device = right
        return pltpu.make_async_remote_copy(
            src_ref=source,
            dst_ref=target,
            send_sem=send_sem.at[slot, half],
            recv_sem=recv_sem.at[slot, 1 - half],
            device_id={"wall": device},
            device_id_type=MESH,
        )

    def exists(half):
        return has_left if half == 0 else has_right

    def send(slot, half, rows):
        @pl.when(exists(half))
        def _():
            halo_copy(slot, half, rows).start()

    def wait_halo(slot, half, rows):
        @pl.when(exists(half))
        def _():
            halo_copy(slot, 1 - half, rows).wait_recv()

    def own(half):
        return pl.ds(half * LAYER, LAYER)

    def put(slot, half, row, value):
        ext_ref[slot, pl.ds(LAYER + half * LAYER, LAYER), pl.ds(row * width, width)] = value

    def get(slot, half, row):
        return ext_ref[slot, pl.ds(LAYER + half * LAYER, LAYER), pl.ds(row * width, width)].astype(F32)

    @pl.when(jnp.logical_not(has_left))
    def _():
        for slot in range(slots):
            ext_ref[slot, pl.ds(0, LAYER), :] = jnp.zeros((LAYER, 4 * width), BF16)

    @pl.when(jnp.logical_not(has_right))
    def _():
        for slot in range(slots):
            ext_ref[slot, pl.ds(3 * LAYER, LAYER), :] = jnp.zeros((LAYER, 4 * width), BF16)

    def finish_nodes(step, carry):
        node_arrival(step).wait()
        return carry

    lax.fori_loop(1, peers, finish_nodes, 0)

    landed_ref[...] = jnp.zeros(landed_ref.shape, F32)

    def scatter_batch(step, carry):
        rows = arrive_ref[pl.ds(step * batch, batch), :]
        slot_ids = lax.broadcasted_iota(jnp.int32, (1, capacity), 1)
        index = jnp.concatenate(
            [
                jnp.where(slot_ids < count_ref[0, step * batch + i], rows[i : i + 1, :], nodes)
                for i in range(batch)
            ],
            axis=1,
        )
        values = jnp.concatenate(
            [in_buf[step * batch + i][0:6, 0:capacity] for i in range(batch)], axis=1
        )
        high, low = split(values)
        parts = [high.astype(F32), low.astype(F32)]
        of_node = lax.broadcasted_iota(jnp.int32, (width, lane_count), 0) == (index & (width - 1))
        of_block = lax.broadcasted_iota(jnp.int32, (blocks, lane_count), 0) == (index >> shift)
        column = jnp.where(of_node, 1.0, 0.0).astype(BF16)
        for row in range(6):
            for k in range(2):
                spread_ref[pl.ds((2 * row + k) * blocks, blocks), :] = jnp.where(
                    of_block, parts[k][row : row + 1, :], 0.0
                ).astype(BF16)
        spread_ref[pl.ds(12 * blocks, blocks), :] = jnp.where(of_block, 1.0, 0.0).astype(BF16)
        landed_ref[...] = landed_ref[...] + lax.dot_general(
            spread_ref[...], column, (((1,), (1,)), ((), ())), preferred_element_type=F32
        )
        return carry

    lax.fori_loop(0, peers // batch, scatter_batch, 0)

    for half in (0, 1):
        hit = landed_ref[pl.ds(12 * blocks + half * LAYER, LAYER), :] > 0.5
        for row in range(6):
            high = landed_ref[pl.ds(2 * row * blocks + half * LAYER, LAYER), :]
            low = landed_ref[pl.ds((2 * row + 1) * blocks + half * LAYER, LAYER), :]
            value = jnp.where(hit, high + low, state[row][row % 3, own(half), :])
            if row < 3:
                pos_ref[row, own(half), :] = value
                put(0, half, row, value.astype(BF16))
            else:
                vel_ref[row - 3, own(half), :] = value
        send(0, half, 3)

    group = 9 if nnz % 9 == 0 else nnz

    def contract(slot, rows, half):
        wide = rows * width
        source = ext_ref[slot, pl.ds(half * LAYER, reach), pl.ds(0, wide)]
        for start in range(0, nnz, group):
            part = pl.ds(start * LAYER, group * LAYER)
            picked_ref[part, pl.ds(0, wide)] = jnp.dot(
                onehot_ref[half, part, :], source, preferred_element_type=F32
            ).astype(BF16)
        sums = [jnp.zeros((LAYER, width), F32) for _ in range(rows)]
        for j in range(nnz):
            part = pl.ds(j * LAYER, LAYER)
            mask = intact_ref[j, own(half), :]
            stacked = jnp.concatenate(
                [picked_ref[part, pl.ds(row * width, width)] for row in range(rows)], axis=0
            )
            product = jnp.dot(stacked, wt_ref[j], preferred_element_type=F32)
            for row in range(rows):
                sums[row] = sums[row] + product[row * LAYER : (row + 1) * LAYER] * mask
        return sums

    def evaluation(t, carry):
        near, far = 2 * t, 2 * t + 1
        for half in (0, 1):
            wait_halo(near, half, 3)
            summed = contract(near, 3, half)
            scaling = mod_ref[own(half), :]
            stiffness = stiff_ref[own(half), :]
            rounded = [get(near, half, row) for row in range(3)]
            stretch = [scaling * (summed[row] - stiffness * rounded[row]) for row in range(3)]
            dilatation = (stretch[0] + stretch[1] + stretch[2]) / 3.0
            soften = 1.0 / (1.0 + dilatation * dilatation)
            soft_low = soften.astype(BF16)
            soft_wide = soft_low.astype(F32)
            for row in range(3):
                put(far, half, row, (soft_wide * rounded[row]).astype(BF16))
                stretch_ref[row, own(half), :] = stretch[row]
            put(far, half, 3, soft_low)
            soften_ref[own(half), :] = soften
            send(far, half, 4)
        for half in (1, 0):
            wait_halo(far, half, 4)
            paired = contract(far, 4, half)
            scaling = mod_ref[own(half), :]
            soften = soften_ref[own(half), :]
            for row in range(3):
                rounded = get(near, half, row)
                force = 0.5 * (
                    scaling * (paired[row] - rounded * paired[3]) + soften * stretch_ref[row, own(half), :]
                )

                @pl.when(t > 0)
                def _():
                    vel_ref[row, own(half), :] = vel_ref[row, own(half), :] + 0.5 * TIME_STEP * (
                        acc_ref[row, own(half), :] + force
                    )

                acc_ref[row, own(half), :] = force

            @pl.when(t < SUBSTEPS)
            def _():
                for row in range(3):
                    moved = (
                        pos_ref[row, own(half), :]
                        + TIME_STEP * vel_ref[row, own(half), :]
                        + 0.5 * TIME_STEP * TIME_STEP * acc_ref[row, own(half), :]
                    )
                    pos_ref[row, own(half), :] = moved
                    put(2 * t + 2, half, row, moved.astype(BF16))
                send(2 * t + 2, half, 3)

        return carry

    lax.fori_loop(0, SUBSTEPS + 1, evaluation, 0)

    for half in range(2):
        @pl.when(exists(half))
        def _():
            for slot in range(slots):
                halo_copy(slot, half, 3 if slot % 2 == 0 else 4).wait_send()


def shards(
    displacement,
    velocity,
    send_list,
    arrive_list,
    recv_count,
    horizon_blocks,
    bond_intact,
    modulus,
    bond_weight,
):
    node_count = displacement.shape[1]
    blocks, nnz, width = bond_intact.shape
    peers, capacity = send_list.shape[1:]
    lane_count = math.gcd(PEER_BATCH, peers) * capacity
    slots = 2 * (SUBSTEPS + 1)
    vmem = pl.BlockSpec(memory_space=pltpu.VMEM)
    hbm = pl.BlockSpec(memory_space=pltpu.HBM)
    shape = jax.ShapeDtypeStruct((3, blocks, width), F32)
    final_position, final_speed = pl.pallas_call(
        functools.partial(force_kernel, blocks, width, nnz, peers),
        out_shape=(shape, shape),
        in_specs=[hbm] * 9,
        out_specs=(vmem, vmem),
        scratch_shapes=[
            pltpu.VMEM((peers, capacity), jnp.int32),
            pltpu.VMEM((peers, capacity), jnp.int32),
            pltpu.SMEM((1, peers), jnp.int32),
            pltpu.VMEM((nnz, blocks), jnp.int32),
            pltpu.VMEM((blocks, width), F32),
            pltpu.VMEM((nnz, width, width), BF16),
            pltpu.VMEM((blocks, 3, width), F32),
            pltpu.VMEM((blocks, 3, width), F32),
            pltpu.VMEM((3, blocks, width), F32),
            pltpu.VMEM((3, blocks, width), F32),
            pltpu.VMEM((peers, 8, 128 * pl.cdiv(capacity, 128)), F32),
            pltpu.VMEM((peers, 8, 128 * pl.cdiv(capacity, 128)), F32),
            pltpu.VMEM((13 * blocks, lane_count), BF16),
            pltpu.VMEM((13 * blocks, width), F32),
            pltpu.VMEM((nnz, blocks, width), jnp.int32),
            pltpu.VMEM((nnz, blocks, width), F32),
            pltpu.VMEM((nnz, width, width), BF16),
            pltpu.VMEM((2, nnz * LAYER, 3 * LAYER), BF16),
            pltpu.VMEM((slots, 4 * LAYER, 4 * width), BF16),
            pltpu.VMEM((nnz * LAYER, 4 * width), BF16),
            pltpu.VMEM((blocks, width), F32),
            pltpu.VMEM((3, blocks, width), F32),
            pltpu.VMEM((3, blocks, width), F32),
            pltpu.VMEM((blocks, width), F32),
            pltpu.SemaphoreType.DMA((slots, 2)),
            pltpu.SemaphoreType.DMA((slots, 2)),
            pltpu.SemaphoreType.DMA((peers,)),
            pltpu.SemaphoreType.DMA((peers,)),
            pltpu.SemaphoreType.DMA((9,)),
        ],
        compiler_params=pltpu.CompilerParams(
            collective_id=0, has_side_effects=True, vmem_limit_bytes=67043328
        ),
        name="forces",
    )(
        send_list,
        arrive_list,
        recv_count,
        jnp.transpose(horizon_blocks),
        jnp.transpose(bond_intact, (1, 0, 2)),
        modulus.reshape(blocks, width),
        bond_weight,
        jnp.transpose(displacement.reshape(3, blocks, width), (1, 0, 2)),
        jnp.transpose(velocity.reshape(3, blocks, width), (1, 0, 2)),
    )
    return (final_position.reshape(3, node_count), final_speed.reshape(3, node_count))


def solution(mesh):
    in_specs = (
        P(None, ("parts", "wall")),
        P(None, ("parts", "wall")),
        P(("parts", "wall"), None, None),
        P(("parts", "wall"), None, None),
        P(("parts", "wall"), None),
        P(("parts", "wall"), None),
        P(("parts", "wall"), None, None),
        P(("parts", "wall")),
        P(),
    )
    out_specs = (P(None, ("parts", "wall")), P(None, ("parts", "wall")))
    return jax.shard_map(shards, mesh=mesh, in_specs=in_specs, out_specs=out_specs, check_vma=False)
```
